32 devices in a mesh: dp: 8 (over z, core), tensor: 4 (over y, x).
Axes of the slice: x: 2, y: 2, z: 4, core: 2. Of those that a mesh axis runs over, the one named last changes fastest.
Arguments:
- out_grad: bfloat16 [8192, 1024], P('dp'), may hold values from -6 to 6
- hidden: bfloat16 [8192, 8192], P('dp', 'tensor'), may hold values from -6 to 6
- error_buffer: bfloat16 [8192, 8192], P('dp', 'tensor'), may hold values from -6 to 6
- right_factor: float32 [8192, 64], P('tensor'), may hold values from -6 to 6
Outputs:
- error_next: bfloat16 [8192, 8192], P('dp', 'tensor')
- factor_next: float32 [8192, 64], P('tensor')
The draws below stay inside these ranges and needn't reach their ends.
All inputs are finite; a program needn't handle non-finite values.
Results may differ from the reference program's by a relative error of at most 0.001.
Values sent between devices are 32-bit elements; how exact they have to be, the bound alone decides.
No kernel may reach another device: no remote copies, remote signals or barrier semaphores. Data moves between devices by JAX's collectives and lax.ppermute only.
A program may use at most 64 MiB of HBM per device.

```python
import jax
import jax.numpy as jnp
from jax import lax

FF = 8192
R = 1024
RANK = 64
TOK = 1024
TOKENS = 8192
ROWS = 8192
N_DP = 8


def levels(rng, extent, cuts, low, largest):
    loudness = 1.0
    for axis_at, parts in cuts:
        draws = jax.random.uniform(jax.random.fold_in(jax.random.fold_in(rng, 6), axis_at), (parts,), jnp.float32, low / len(cuts), largest / len(cuts))
        loudness = loudness * jnp.repeat(jnp.exp(draws), extent[axis_at] // parts).reshape((-1,) + (1,) * (len(extent) - 1 - axis_at))
    return loudness


def centred(rng, dims, scale, bound, split=(), held_as=jnp.bfloat16):
    values = jax.random.normal(rng, dims, jnp.float32) * scale
    if len(split) > 0:
        values = levels(rng, dims, split, -0.22, 0.18) * values
    return jnp.clip(values, min=-bound, max=bound).astype(held_as)


def setup_inputs(seed: int = 0) -> dict:
    arg_keys = jax.random.split(jax.random.key(seed), 5)
    return {
        "out_grad": centred(arg_keys[0], (TOKENS, R), 1.0, 6.0, ((0, 8),)),
        "hidden": centred(arg_keys[1], (TOKENS, FF), 1.0, 6.0, ((0, 8), (1, 4))),
        "error_buffer": centred(arg_keys[2], (ROWS, FF), 1.0, 6.0, ((0, 8), (1, 4))),
        "right_factor": centred(arg_keys[3], (FF, RANK), 1.0, 6.0, ((0, 4),), jnp.float32),
    }


def orthonormalize(matrix):
    width = matrix.shape[1]

    def one_column(column_index, basis):
        column = lax.dynamic_slice_in_dim(basis, column_index, 1, 1)
        column = column / jnp.sqrt(jnp.sum(column * column))
        later_mask = (jnp.arange(width) > column_index).astype(basis.dtype)
        correlation = jnp.dot(column.T, basis, precision=lax.Precision.HIGHEST)
        basis = basis - column * (correlation * later_mask)
        return lax.dynamic_update_slice_in_dim(basis, column, column_index, 1)
    return lax.fori_loop(0, width, one_column, matrix)

def reference(out_grad, hidden, error_buffer, right_factor):
    tok_scale = TOK ** (-0.5)
    grads_rep = out_grad.reshape(N_DP, TOK, R)
    hidden_rep = hidden.reshape(N_DP, TOK, FF)
    errors_rep = error_buffer.reshape(N_DP, R, FF)

    def merge_one(pieces):
        grad_piece, hidden_piece, error_piece = pieces
        gradient = lax.dot_general(grad_piece, hidden_piece, (((0,), (0,)), ((), ())), preferred_element_type=jnp.float32)
        return gradient * tok_scale + error_piece.astype(jnp.float32)
    merged = lax.map(merge_one, (grads_rep, hidden_rep, errors_rep))

    def add_left(running, matrix):
        return (running + jnp.dot(matrix, right_factor, precision=lax.Precision.HIGHEST), None)
    left_sum, _ = lax.scan(add_left, jnp.zeros((R, RANK), jnp.float32), merged)
    basis = orthonormalize(left_sum)

    def add_right(running, matrix):
        return (running + jnp.dot(matrix.T, basis, precision=lax.Precision.HIGHEST), None)
    right_sum, _ = lax.scan(add_right, jnp.zeros((FF, RANK), jnp.float32), merged)
    factor_next = right_sum / N_DP
    approx = jnp.dot(basis, factor_next.T, precision=lax.Precision.HIGHEST)

    def update_one(matrix):
        return (matrix - approx).astype(jnp.bfloat16)
    error_next = lax.map(update_one, merged).reshape(N_DP * R, FF)
    return (error_next, factor_next)
```

```python
import functools

import jax
import jax.numpy as jnp
from jax import lax
from jax.experimental import pallas as pl
from jax.experimental.pallas import tpu as pltpu
from jax.sharding import PartitionSpec as P

F32 = jnp.float32
BF16 = jnp.bfloat16
AXES = ("dp", "tensor")
HIGHEST = lax.Precision.HIGHEST


def halves(value):
    high = value.astype(BF16)
    return high, (value - high.astype(F32)).astype(BF16)


def dot(left, right, dims=(1, 0), precision=None):
    return lax.dot_general(
        left,
        right,
        (((dims[0],), (dims[1],)), ((), ())),
        precision=precision,
        preferred_element_type=F32,
    )


def low_lanes(shape, rank):
    return lax.broadcasted_iota(jnp.int32, shape, 1) < rank


def merge_kernel(scale, rank, rows_at_once, grad_ref, hid_ref, err_ref, rt_ref,
                 high_ref, low_ref, left_ref, gt_ref, acc_ref):
    step = pl.program_id(0)
    rows = gt_ref.shape[0]

    @pl.when(step == 0)
    def _():
        for at in range(0, rows, rows_at_once):
            gt_ref[at : at + rows_at_once, :] = grad_ref[:, at : at + rows_at_once].T
        acc_ref[...] = jnp.zeros_like(acc_ref)

    r_high, r_low = halves(rt_ref[...])
    r_both = jnp.concatenate([r_high, r_low], axis=0)
    for at in range(0, rows, rows_at_once):
        here = slice(at, at + rows_at_once)
        gradient = dot(gt_ref[here, :], hid_ref[...])
        merged = gradient * scale + err_ref[here, :].astype(F32)
        high, low = halves(merged)
        high_ref[here, :] = high
        low_ref[here, :] = low
        acc_ref[here, :] += dot(high, r_both, (1, 1)) + dot(low, r_both, (1, 1))

    @pl.when(step == pl.num_programs(0) - 1)
    def _():
        left = acc_ref[...]
        left = left + pltpu.roll(left, rank, 1)
        half = rows // 2
        first = low_lanes((half, 2 * rank), rank)
        left_ref[...] = jnp.where(first, left[:half], left[half:])


def merge(out_grad, hidden, error_buffer, right_t, tile):
    tok, rows = out_grad.shape
    columns = hidden.shape[1]
    rank = right_t.shape[0]
    return pl.pallas_call(
        functools.partial(merge_kernel, tok ** (-0.5), rank, min(256, rows)),
        grid=(columns // tile,),
        in_specs=[
            pl.BlockSpec((tok, rows), lambda j: (0, 0), pipeline_mode=pl.Buffered(1)),
            pl.BlockSpec((tok, tile), lambda j: (0, j)),
            pl.BlockSpec((rows, tile), lambda j: (0, j)),
            pl.BlockSpec((rank, tile), lambda j: (0, j)),
        ],
        out_specs=[
            pl.BlockSpec((rows, tile), lambda j: (0, j)),
            pl.BlockSpec((rows, tile), lambda j: (0, j)),
            pl.BlockSpec((rows // 2, 2 * rank), lambda j: (0, 0)),
        ],
        out_shape=[
            jax.ShapeDtypeStruct((rows, columns), BF16),
            jax.ShapeDtypeStruct((rows, columns), BF16),
            jax.ShapeDtypeStruct((rows // 2, 2 * rank), F32),
        ],
        scratch_shapes=[pltpu.VMEM((rows, tok), BF16), pltpu.VMEM((rows, 2 * rank), F32)],
        compiler_params=pltpu.CompilerParams(vmem_limit_bytes=32 << 20),
        name="merge",
    )(out_grad, hidden, error_buffer, right_t)


def right_kernel(rank, left_ref, high_ref, low_ref, out_ref, lt_ref):
    @pl.when(pl.program_id(0) == 0)
    def _():
        both = left_ref[...].T
        left_t = jnp.concatenate([both[:rank], both[rank:]], axis=1)
        high, low = halves(left_t)
        lt_ref[:rank, :] = high
        lt_ref[rank:, :] = low

    terms = dot(lt_ref[...], high_ref[...]) + dot(lt_ref[...], low_ref[...])
    out_ref[...] = terms[:rank] + terms[rank:]


def right_terms(left, high, low, rank, tile):
    rows, columns = high.shape
    return pl.pallas_call(
        functools.partial(right_kernel, rank),
        grid=(columns // tile,),
        in_specs=[
            pl.BlockSpec(left.shape, lambda j: (0, 0), pipeline_mode=pl.Buffered(1)),
            pl.BlockSpec((rows, tile), lambda j: (0, j)),
            pl.BlockSpec((rows, tile), lambda j: (0, j)),
        ],
        out_specs=pl.BlockSpec((rank, tile), lambda j: (0, j)),
        out_shape=jax.ShapeDtypeStruct((rank, columns), F32),
        scratch_shapes=[pltpu.VMEM((2 * rank, rows), BF16)],
        compiler_params=pltpu.CompilerParams(vmem_limit_bytes=16 << 20),
        name="right_terms",
    )(left, high, low)


def factor_kernel(rank, left_ref, out_ref):
    left = left_ref[...]
    gram = dot(left, left, (0, 0), HIGHEST)
    gram = gram[:rank, :rank] + gram[rank:, rank:]
    row = lax.broadcasted_iota(jnp.int32, (rank, 1), 0)
    eye = (
        lax.broadcasted_iota(jnp.int32, (rank, rank), 0)
        == lax.broadcasted_iota(jnp.int32, (rank, rank), 1)
    ).astype(F32)
    work = jnp.concatenate([gram, eye], axis=1)
    for k in range(rank):
        scale = lax.rsqrt(work[k : k + 1, k : k + 1])
        pivot = work[k : k + 1, :] * scale
        column = work[:, k : k + 1] * scale
        work = jnp.where(row > k, work - column * pivot, work)
        work = jnp.where(row == k, pivot, work)
    out_ref[...] = work[:, rank:]


def factor(left, rank):
    return pl.pallas_call(
        functools.partial(factor_kernel, rank),
        out_shape=jax.ShapeDtypeStruct((rank, rank), F32),
        compiler_params=pltpu.CompilerParams(vmem_limit_bytes=8 << 20),
        name="factor",
    )(left)


def finish_kernel(rank, replicas, rows_at_once, left_ref, inverse_ref, sum_ref, high_ref,
                  low_ref, error_ref, next_ref, lp_ref):
    rows = high_ref.shape[0]

    @pl.when(pl.program_id(0) == 0)
    def _():
        half = rows // 2
        left = left_ref[...]
        first = low_lanes(left.shape, rank)
        other = pltpu.roll(left, rank, 1)
        for at, mine in ((0, left), (half, other)):
            high, low = halves(mine)
            moved = pltpu.roll(low.astype(F32), rank, 1)
            lp_ref[at : at + half, : 2 * rank] = jnp.where(first, high.astype(F32), moved).astype(BF16)
            lp_ref[at : at + half, 2 * rank :] = jnp.where(first, high.astype(F32), 0.0).astype(BF16)

    inverse = inverse_ref[...]
    factor_next = dot(inverse, sum_ref[...], (1, 0), HIGHEST) * (1.0 / replicas)
    next_ref[...] = factor_next
    weight = dot(inverse, factor_next, (0, 0), HIGHEST)
    high, low = halves(weight)
    weights = jnp.concatenate([high, high, low, jnp.zeros_like(low)], axis=0)
    for at in range(0, rows, rows_at_once):
        here = slice(at, at + rows_at_once)
        approx = dot(lp_ref[here, :], weights)
        merged = high_ref[here, :].astype(F32) + low_ref[here, :].astype(F32)
        error_ref[here, :] = (merged - approx).astype(BF16)


def finish(left, inverse, right_sum, high, low, replicas, tile):
    rows, columns = high.shape
    rank = inverse.shape[0]
    return pl.pallas_call(
        functools.partial(finish_kernel, rank, replicas, min(256, rows)),
        grid=(columns // tile,),
        in_specs=[
            pl.BlockSpec(left.shape, lambda j: (0, 0), pipeline_mode=pl.Buffered(1)),
            pl.BlockSpec(inverse.shape, lambda j: (0, 0), pipeline_mode=pl.Buffered(1)),
            pl.BlockSpec((rank, tile), lambda j: (0, j)),
            pl.BlockSpec((rows, tile), lambda j: (0, j)),
            pl.BlockSpec((rows, tile), lambda j: (0, j)),
        ],
        out_specs=[
            pl.BlockSpec((rows, tile), lambda j: (0, j)),
            pl.BlockSpec((rank, tile), lambda j: (0, j)),
        ],
        out_shape=[
            jax.ShapeDtypeStruct((rows, columns), BF16),
            jax.ShapeDtypeStruct((rank, columns), F32),
        ],
        scratch_shapes=[pltpu.VMEM((rows, 4 * rank), BF16)],
        compiler_params=pltpu.CompilerParams(vmem_limit_bytes=24 << 20),
        name="finish",
    )(left, inverse, right_sum, high, low)


def exchange(value, mask, devices):
    return lax.ppermute(value, AXES, [(i, i ^ mask) for i in range(devices)])


def scatter_half(value, mask, devices, upper):
    half = value.shape[0] // 2
    keep = jnp.where(upper, value[half:], value[:half])
    give = jnp.where(upper, value[:half], value[half:])
    return keep + exchange(give, mask, devices)


def gather_half(value, mask, devices, upper):
    other = exchange(value, mask, devices)
    return jnp.concatenate(
        [jnp.where(upper, other, value), jnp.where(upper, value, other)], axis=0
    )


def bits(start, stop):
    masks = []
    while start < stop:
        masks.append(start)
        start *= 2
    return masks


def all_sum(value, scattered, exchanged, devices):
    where = lax.axis_index(AXES)
    upper = [(where & mask) != 0 for mask in scattered]
    for mask, up in zip(scattered, upper):
        value = scatter_half(value, mask, devices, up)
    for mask in exchanged:
        value = value + exchange(value, mask, devices)
    for mask, up in reversed(list(zip(scattered, upper))):
        value = gather_half(value, mask, devices, up)
    return value


def body(out_grad, hidden, error_buffer, right_factor):
    replicas, shards = lax.axis_size("dp"), lax.axis_size("tensor")
    devices = replicas * shards
    rank = right_factor.shape[1]
    tile = 256
    high, low, left = merge(out_grad, hidden, error_buffer, right_factor.T, tile)
    tensor_bits, dp_bits = bits(1, shards), bits(shards, devices)
    left = all_sum(left, [dp_bits[0], tensor_bits[0]], tensor_bits[1:] + dp_bits[1:], devices)
    right_sum = right_terms(left, high, low, rank, tile)
    inverse = factor(left, rank)
    right_sum = all_sum(right_sum, dp_bits[:2], dp_bits[2:], devices)
    error_next, factor_next = finish(left, inverse, right_sum, high, low, replicas, tile)
    return (error_next, factor_next.T)


def solution(mesh):
    placed = (P("dp", None), P("dp", "tensor"), P("dp", "tensor"), P("tensor", None))
    return jax.shard_map(
        body,
        mesh=mesh,
        in_specs=placed,
        out_specs=(P("dp", "tensor"), P("tensor", None)),
        check_vma=False,
    )
```
